1024 devices in a mesh: seq: 64 (over y, x, z_hi, core), head: 16 (over z_lo).
Axes of the slice: x: 4, y: 4, z: 32 (z_hi: 2, z_lo: 16; z = z_hi * 16 + z_lo), core: 2. Of those that a mesh axis runs over, the one named last changes fastest.
Arguments:
- queries: bfloat16 [16384, 8192], P(('seq', 'head')), may hold values from -0.125 to 0.125
- key_rows: bfloat16 [16384, 8192], P(('seq', 'head')), may hold values from -0.125 to 0.125
- value_rows: bfloat16 [16384, 8192], P(('seq', 'head')), may hold values from -0.125 to 0.125
- out_grad: bfloat16 [16384, 8192], P(('seq', 'head')), may hold values from -6 to 6
- log_decay: float32 [64, 16384], P('head', 'seq'), may hold values from -0.9 to 0, as said below
Outputs:
- query_grad: bfloat16 [16384, 8192], P(('seq', 'head'))
- key_grad: bfloat16 [16384, 8192], P(('seq', 'head'))
- value_grad: bfloat16 [16384, 8192], P(('seq', 'head'))
The draws below stay inside these ranges and needn't reach their ends.
Inputs may be any that keep to these rules, and one draw needn't show every extreme that they name: `log_decay`: never positive.
All inputs are finite; a program needn't handle non-finite values.
Results may differ from the reference program's by a relative error of at most 0.0057.
Values may be sent and summed in bfloat16 or wider, within the bound.
A program may use at most 128 MiB of HBM per device.

```python
import jax
import jax.numpy as jnp
from jax import lax

HEAD_COUNT = 64
HEAD_DIM = 128
BLOCK = 256
SEG_DEV = 256
TOKEN_COUNT = 16384


def draw_log_decay(key, part):
    every_key = jax.random.split(key, 7)
    fast_share = 0.5
    fast_heads = jax.random.uniform(every_key[0], (HEAD_COUNT, 1)) < fast_share
    fast_rate = jax.random.uniform(every_key[1], (HEAD_COUNT, 1), jnp.float32, 1.0 / 50.0, 1.0 / 30.0)
    slow_rate = jax.random.uniform(every_key[2], (HEAD_COUNT, 1), jnp.float32, 0.25, 1.0) * 0.5 / TOKEN_COUNT
    head_decay_rate = jnp.where(fast_heads, fast_rate, slow_rate)
    coarse_estimate = jnp.exp(jax.random.uniform(every_key[3], (HEAD_COUNT, TOKEN_COUNT), jnp.float32, -0.69, 0.69))
    regions = TOKEN_COUNT // SEG_DEV
    segment_multiplier = jnp.exp(jax.random.uniform(every_key[4], (HEAD_COUNT, regions, 1), jnp.float32, -0.69, 0.69))
    segment_multiplier = jnp.broadcast_to(segment_multiplier, (HEAD_COUNT, regions, SEG_DEV)).reshape(HEAD_COUNT, TOKEN_COUNT)
    spike_position = jax.random.randint(every_key[5], (HEAD_COUNT, 2), 0, TOKEN_COUNT)
    token_positions = jnp.arange(TOKEN_COUNT)
    spike_applied = jnp.any(token_positions[None, :, None] == spike_position[:, None, :], axis=-1)
    spike_magnitude = jax.random.uniform(every_key[6], (HEAD_COUNT, TOKEN_COUNT), jnp.float32, 0.2, 0.5)
    spike_log_decay = jnp.where(spike_applied, jnp.log(1.0 - spike_magnitude), 0.0)
    return (-head_decay_rate * coarse_estimate * segment_multiplier + spike_log_decay).astype(jnp.float32)


def levels(stream_key, dims, cuts, low, high):
    factor_of = 1.0
    for dim, parts in cuts:
        steps = jax.random.uniform(jax.random.fold_in(jax.random.fold_in(stream_key, 6), dim), (parts,), jnp.float32, low / len(cuts), high / len(cuts))
        factor_of = factor_of * jnp.repeat(jnp.exp(steps), dims[dim] // parts).reshape((-1,) + (1,) * (len(dims) - 1 - dim))
    return factor_of


def centred(own_key, extent, scale, most, cuts=(), kind=jnp.bfloat16):
    values = jax.random.normal(own_key, extent, jnp.float32) * scale
    if len(cuts) > 0:
        values = levels(own_key, extent, cuts, -0.22, 0.18) * values
    return jnp.clip(values, min=-most, max=most).astype(kind)


def setup_inputs(seed: int = 0) -> dict:
    splits = jax.random.split(jax.random.key(seed), 6)
    queries = centred(splits[0], (TOKEN_COUNT, HEAD_COUNT * HEAD_DIM), (16 * HEAD_DIM) ** -0.5, 0.125, ((0, 1024),))
    key_rows = centred(splits[1], (TOKEN_COUNT, HEAD_COUNT * HEAD_DIM), (16 * HEAD_DIM) ** -0.5, 0.125, ((0, 1024),))
    value_rows = centred(splits[2], (TOKEN_COUNT, HEAD_COUNT * HEAD_DIM), (16 * HEAD_DIM) ** -0.5, 0.125, ((0, 1024),))
    out_grad = centred(splits[3], (TOKEN_COUNT, HEAD_COUNT * HEAD_DIM), 1.0, 6.0, ((0, 1024),))
    log_decay = draw_log_decay(jax.random.fold_in(splits[5], 71), 0)
    return dict(queries=queries, key_rows=key_rows, value_rows=value_rows, out_grad=out_grad, log_decay=log_decay)


def as_float(array):
    return array.astype(jnp.float32)


def scaled_rows(rows, weight):
    return (rows.astype(jnp.float32) * weight[..., None]).astype(jnp.bfloat16)


def one_head(operands):
    query_block, key_block, value_block, grad_block, decay_row = operands
    nblocks = TOKEN_COUNT // BLOCK
    query_block = query_block.reshape(nblocks, BLOCK, HEAD_DIM)
    key_block = key_block.reshape(nblocks, BLOCK, HEAD_DIM)
    value_block = value_block.reshape(nblocks, BLOCK, HEAD_DIM)
    grad_block = grad_block.reshape(nblocks, BLOCK, HEAD_DIM)
    cumulative = jnp.cumsum(decay_row.reshape(nblocks, BLOCK), axis=1)
    last_value = cumulative[:, -1:]
    query_weight = jnp.exp(cumulative)
    key_weight = jnp.exp(last_value - cumulative)
    block_gate = jnp.exp(last_value[:, 0])
    key_scaled = scaled_rows(key_block, key_weight)
    query_scaled = scaled_rows(query_block, query_weight)
    block_state = jnp.einsum("nbi,nbj->nij", as_float(key_scaled), as_float(value_block))
    block_grad = jnp.einsum("nbi,nbj->nij", as_float(query_scaled), as_float(grad_block))

    def advance(running, element):
        gate_now, state_now = element
        return gate_now * running + state_now, running

    zero_state = jnp.zeros((HEAD_DIM, HEAD_DIM), jnp.float32)
    _, state_in = lax.scan(advance, zero_state, (block_gate, block_state))
    _, state_out = lax.scan(advance, zero_state, (block_gate, block_grad), reverse=True)
    state_in_low = state_in.astype(jnp.bfloat16)
    state_out_low = state_out.astype(jnp.bfloat16)
    token_positions = jnp.arange(BLOCK)
    causal = token_positions[:, None] >= token_positions[None, :]
    spread_log = cumulative[:, :, None] - cumulative[:, None, :]
    decay_matrix = jnp.where(causal, jnp.exp(jnp.where(causal, spread_log, 0.0)), 0.0)
    grad_scores = (jnp.einsum("nti,nsi->nts", as_float(grad_block), as_float(value_block)) * decay_matrix).astype(jnp.bfloat16)
    scores = (jnp.einsum("nti,nsi->nts", as_float(query_block), as_float(key_block)) * decay_matrix).astype(jnp.bfloat16)
    query_grad = jnp.einsum("nts,nsi->nti", as_float(grad_scores), as_float(key_block))
    query_grad = query_grad + query_weight[..., None] * jnp.einsum("ntj,nij->nti", as_float(grad_block), as_float(state_in_low))
    key_grad = jnp.einsum("nts,nti->nsi", as_float(grad_scores), as_float(query_block))
    key_grad = key_grad + key_weight[..., None] * jnp.einsum("nsj,nij->nsi", as_float(value_block), as_float(state_out_low))
    value_grad = jnp.einsum("nts,ntj->nsj", as_float(scores), as_float(grad_block))
    value_grad = value_grad + key_weight[..., None] * jnp.einsum("nsi,nij->nsj", as_float(key_block), as_float(state_out_low))
    return (query_grad.reshape(TOKEN_COUNT, HEAD_DIM).astype(jnp.bfloat16),
            key_grad.reshape(TOKEN_COUNT, HEAD_DIM).astype(jnp.bfloat16),
            value_grad.reshape(TOKEN_COUNT, HEAD_DIM).astype(jnp.bfloat16))


def by_head(array):
    return array.reshape(TOKEN_COUNT, HEAD_COUNT, HEAD_DIM).transpose(1, 0, 2)


def by_token(array):
    return array.transpose(1, 0, 2).reshape(TOKEN_COUNT, HEAD_COUNT * HEAD_DIM)


def reference(queries, key_rows, value_rows, out_grad, log_decay):
    query_grad, key_grad, value_grad = lax.map(
        one_head, (by_head(queries), by_head(key_rows), by_head(value_rows), by_head(out_grad), log_decay))
    return (by_token(query_grad), by_token(key_grad), by_token(value_grad))
```

```python
import jax
import jax.numpy as jnp
from jax import lax
from jax.experimental import pallas as pl
from jax.experimental.pallas import tpu as pltpu
from jax.sharding import PartitionSpec as P

MESH = pl.DeviceIdType.MESH
F32 = jnp.float32
BF16 = jnp.bfloat16

DIM = 128
BLOCK = 256
ROWS = 16
LINE = 16
RING = 32
SIDE = 4
BLOCKS = 4
HEADS = 64
SLOTS = RING * 2
STATE = DIM + 8

K, V, G, Q = 0, 1, 2, 3
DQ, DK, DV = 0, 1, 2


def nt(a, b):
    return lax.dot_general(a, b, (((1,), (1,)), ((), ())), preferred_element_type=F32)


def nn(a, b):
    return lax.dot_general(a, b, (((1,), (0,)), ((), ())), preferred_element_type=F32)


def tn(a, b):
    return lax.dot_general(a, b, (((0,), (0,)), ((), ())), preferred_element_type=F32)


def kernel(
    q_in, k_in, v_in, g_in, decay_in, dq_out, dk_out, dv_out,
    stage, decay_own, decays, rows, back, result,
    decay_matrix, query_weight, key_weight, gates, scores,
    states, before, part_dk, part_dv,
    total_out, gather_x, row_out, gather_y,
    stage_sem, decay_sem, in_send, in_recv, out_send, out_recv, scan_send, scan_recv, final_sem,
):
    s, z_lo = lax.axis_index("seq"), lax.axis_index("head")
    y, x, z_hi, core = s // 16, (s // 4) % 4, (s // 2) % 2, s % 2
    base = (s // 4) * 4
    z = z_hi * LINE + z_lo
    my_block = z_hi * 2 + core
    my_slot = my_block * LINE + z_lo
    my_head = z_lo * BLOCKS + my_block

    def device(zz, cc):
        return (base + (zz // LINE) * 2 + cc, zz % LINE)

    def slot_of(zz, cc):
        return ((zz // LINE) * 2 + cc) * LINE + zz % LINE

    def head_of(zz, cc):
        return (zz % LINE) * BLOCKS + (zz // LINE) * 2 + cc

    def slot_rows(slot):
        return pl.ds(pl.multiple_of(slot * ROWS, ROWS), ROWS)

    def head_cols(head):
        return pl.ds(pl.multiple_of(head * DIM, DIM), DIM)

    sources = (k_in, v_in, g_in, q_in)
    for t in range(4):
        pltpu.make_async_copy(sources[t], stage.at[t], stage_sem.at[t]).start()
    decay_load = pltpu.make_async_copy(decay_in, decay_own, stage_sem.at[4])
    decay_load.start()

    barrier = pltpu.get_barrier_semaphore()

    def greet(i, carry):
        pl.semaphore_signal(
            barrier, inc=1, device_id=device((z + i // 2) % RING, (core + i) % 2), device_id_type=MESH
        )
        return carry

    lax.fori_loop(1, SLOTS, greet, 0)
    for step in range(1, SIDE):
        for peer in (y * 16 + ((x + step) % SIDE) * 4, ((y + step) % SIDE) * 16 + x * 4):
            pl.semaphore_signal(
                barrier, inc=1, device_id=(peer + my_block, z_lo), device_id_type=MESH
            )
    for t in range(4):
        pltpu.make_async_copy(sources[t], stage.at[t], stage_sem.at[t]).wait()
    decay_load.wait()
    pl.semaphore_wait(barrier, SLOTS - 1 + 2 * (SIDE - 1))

    def exchange(send):
        def both_ways(i, carry):
            far = LINE - i
            for cc in (0, 1):
                send((z + far) % RING, cc)

            @pl.when(far < LINE)
            def _():
                for cc in (0, 1):
                    send((z + RING - far) % RING, cc)

            return carry

        lax.fori_loop(0, LINE, both_ways, 0)
        send(z, 1 - core)

    def send_inputs(t):
        def send(zz, cc):
            pltpu.make_async_remote_copy(
                src_ref=stage.at[t].at[:, head_cols(head_of(zz, cc))],
                dst_ref=rows.at[t].at[slot_rows(my_slot)],
                send_sem=in_send.at[t],
                recv_sem=in_recv.at[t],
                device_id=device(zz, cc),
                device_id_type=MESH,
            ).start()

        exchange(send)
        pltpu.make_async_copy(
            stage.at[t].at[:, head_cols(my_head)], rows.at[t].at[slot_rows(my_slot)], in_recv.at[t]
        ).start()

    def send_outputs(t):
        def send(zz, cc):
            pltpu.make_async_remote_copy(
                src_ref=back.at[t].at[slot_rows(slot_of(zz, cc))],
                dst_ref=result.at[t].at[:, head_cols(my_head)],
                send_sem=out_send.at[t],
                recv_sem=out_recv.at[t],
                device_id=device(zz, cc),
                device_id_type=MESH,
            ).start()

        exchange(send)
        pltpu.make_async_copy(
            back.at[t].at[slot_rows(my_slot)], result.at[t].at[:, head_cols(my_head)], out_recv.at[t]
        ).start()

    def arrived(t):
        pltpu.make_async_copy(rows.at[t], rows.at[t], in_recv.at[t]).wait()

    for step in range(1, BLOCKS):
        peer = (my_block + step) % BLOCKS
        pltpu.make_async_remote_copy(
            src_ref=decay_own,
            dst_ref=decays.at[my_block],
            send_sem=decay_sem.at[0],
            recv_sem=decay_sem.at[1],
            device_id=(base + peer, z_lo),
            device_id_type=MESH,
        ).start()
    pltpu.make_async_copy(decay_own, decays.at[my_block], decay_sem.at[1]).start()
    for t in range(4):
        send_inputs(t)

    pltpu.make_async_copy(decays, decays, decay_sem.at[1]).wait()
    every = decays[...]
    wanted = lax.broadcasted_iota(jnp.int32, every.shape, 1) == my_block
    decay_rows = jnp.sum(jnp.where(wanted, every, 0.0), axis=1)
    upper = (
        lax.broadcasted_iota(jnp.int32, (BLOCK, BLOCK), 0)
        <= lax.broadcasted_iota(jnp.int32, (BLOCK, BLOCK), 1)
    ).astype(F32)
    padded = jnp.concatenate([decay_rows, jnp.zeros_like(decay_rows)], axis=0)
    cumulative = jnp.dot(
        padded, upper, preferred_element_type=F32, precision=lax.Precision.HIGHEST
    )
    time_at = lax.broadcasted_iota(jnp.int32, (BLOCK, DIM), 0)
    source_at = lax.broadcasted_iota(jnp.int32, (BLOCK, DIM), 1)
    for b in range(BLOCKS):
        row = cumulative[b : b + 1, :]
        column = jnp.transpose(jnp.broadcast_to(row, (DIM, BLOCK)))
        last = row[:, BLOCK - 1 : BLOCK]
        query_weight[b] = jnp.exp(column)
        key_weight[b] = jnp.exp(last - column)
        gates[b] = jnp.broadcast_to(jnp.exp(last), (8, DIM))
        for half in range(2):
            causal = time_at >= source_at + half * DIM
            spread = column - row[:, half * DIM : (half + 1) * DIM]
            decay_matrix[b, :, half * DIM : (half + 1) * DIM] = jnp.where(
                causal, jnp.exp(jnp.where(causal, spread, 0.0)), 0.0
            )

    def block(t, b):
        return rows[t, pl.ds(pl.multiple_of(b * BLOCK, BLOCK), BLOCK), :]

    def block_states(weight, left, right, which):
        def one(b, carry):
            scaled = (block(left, b).astype(F32) * weight[b]).astype(BF16)
            states[which, b] = tn(scaled, block(right, b))
            return carry

        lax.fori_loop(0, BLOCKS, one, 0)

    def scan_start(which, order):
        running = jnp.zeros((DIM, DIM), F32)
        gate = jnp.ones((8, DIM), F32)
        for b in order:
            here = gates[b]
            before[which, b, :DIM, :] = running
            before[which, b, DIM:, :] = gate
            running = here[:1] * running + states[which, b]
            gate = gate * here
        total_out[which, :DIM, :] = running
        total_out[which, DIM:, :] = gate
        gather_x[which, x, :DIM, :] = running
        gather_x[which, x, DIM:, :] = gate
        for step in range(1, SIDE):
            peer = y * 16 + ((x + step) % SIDE) * 4 + my_block
            pltpu.make_async_remote_copy(
                src_ref=total_out.at[which],
                dst_ref=gather_x.at[which].at[x],
                send_sem=scan_send.at[which].at[0],
                recv_sem=scan_recv.at[which].at[0],
                device_id=(peer, z_lo),
                device_id_type=MESH,
            ).start()

    def combined(gathered, which, place, order, backward):
        pre, pre_gate = jnp.zeros((DIM, DIM), F32), jnp.ones((8, DIM), F32)
        whole, whole_gate = pre, pre_gate
        for j in order:
            state, gate = gathered[which, j, :DIM, :], gathered[which, j, DIM:, :]
            earlier = j > place if backward else j < place
            pre = jnp.where(earlier, gate[:1] * pre + state, pre)
            pre_gate = jnp.where(earlier, gate * pre_gate, pre_gate)
            whole = gate[:1] * whole + state
            whole_gate = gate * whole_gate
        return pre, pre_gate, whole, whole_gate

    def wait_three(gathered, which, stage_index):
        three = gathered.at[which].at[pl.ds(0, SIDE - 1)]
        pltpu.make_async_copy(three, three, scan_recv.at[which].at[stage_index]).wait()

    def scan_finish(which, backward):
        order = tuple(reversed(range(SIDE))) if backward else tuple(range(SIDE))
        wait_three(gather_x, which, 0)
        pre, pre_gate, whole, whole_gate = combined(gather_x, which, x, order, backward)
        row_out[which, :DIM, :] = whole
        row_out[which, DIM:, :] = whole_gate
        gather_y[which, y, :DIM, :] = whole
        gather_y[which, y, DIM:, :] = whole_gate
        for step in range(1, SIDE):
            peer = ((y + step) % SIDE) * 16 + x * 4 + my_block
            pltpu.make_async_remote_copy(
                src_ref=row_out.at[which],
                dst_ref=gather_y.at[which].at[y],
                send_sem=scan_send.at[which].at[1],
                recv_sem=scan_recv.at[which].at[1],
                device_id=(peer, z_lo),
                device_id_type=MESH,
            ).start()
        wait_three(gather_y, which, 1)
        outer, _, _, _ = combined(gather_y, which, y, order, backward)
        return pre_gate[:1] * outer + pre

    arrived(K)
    arrived(V)
    block_states(key_weight, K, V, 0)
    scan_start(0, tuple(range(BLOCKS)))
    incoming = scan_finish(0, False)
    for b in range(BLOCKS):
        states[0, b] = before[0, b, DIM : DIM + 1, :] * incoming + before[0, b, :DIM, :]

    arrived(G)

    def query_block(b, carry):
        grad = block(G, b)
        low = (nt(grad, block(V, b)) * decay_matrix[b]).astype(BF16)
        scores[b] = low
        inner = nn(low, block(K, b))
        outer = query_weight[b] * nt(grad, states[0, b].astype(BF16))
        back[DQ, pl.ds(pl.multiple_of(b * BLOCK, BLOCK), BLOCK), :] = (inner + outer).astype(BF16)
        return carry

    lax.fori_loop(0, BLOCKS, query_block, 0)
    send_outputs(DQ)

    arrived(Q)
    block_states(query_weight, Q, G, 1)
    scan_start(1, tuple(reversed(range(BLOCKS))))

    def inner_block(b, carry):
        query, grad = block(Q, b), block(G, b)
        part_dk[b] = tn(scores[b], query)
        low = (nt(query, block(K, b)) * decay_matrix[b]).astype(BF16)
        part_dv[b] = tn(low, grad)
        return carry

    lax.fori_loop(0, BLOCKS, inner_block, 0)
    outgoing = scan_finish(1, True)
    for b in range(BLOCKS):
        states[1, b] = before[1, b, DIM : DIM + 1, :] * outgoing + before[1, b, :DIM, :]

    def key_block(b, carry):
        low = states[1, b].astype(BF16)
        grad = part_dk[b] + key_weight[b] * nt(block(V, b), low)
        back[DK, pl.ds(pl.multiple_of(b * BLOCK, BLOCK), BLOCK), :] = grad.astype(BF16)
        return carry

    lax.fori_loop(0, BLOCKS, key_block, 0)
    send_outputs(DK)

    def value_block(b, carry):
        low = states[1, b].astype(BF16)
        grad = part_dv[b] + key_weight[b] * nn(block(K, b), low)
        back[DV, pl.ds(pl.multiple_of(b * BLOCK, BLOCK), BLOCK), :] = grad.astype(BF16)
        return carry

    lax.fori_loop(0, BLOCKS, value_block, 0)
    send_outputs(DV)

    outs = (dq_out, dk_out, dv_out)
    for t in range(3):
        pltpu.make_async_copy(result.at[t], result.at[t], out_recv.at[t]).wait()
        pltpu.make_async_copy(result.at[t], outs[t], final_sem.at[t]).start()

    others = pl.ds(0, (SLOTS - 1) * ROWS)
    for t in range(4):
        sent = rows.at[t].at[others]
        pltpu.make_async_copy(sent, sent, in_send.at[t]).wait()
    for t in range(3):
        sent = back.at[t].at[others]
        pltpu.make_async_copy(sent, sent, out_send.at[t]).wait()
    three = decays.at[pl.ds(0, BLOCKS - 1)]
    pltpu.make_async_copy(three, three, decay_sem.at[0]).wait()
    for which in range(2):
        for stage_index, gathered in enumerate((gather_x, gather_y)):
            three = gathered.at[which].at[pl.ds(0, SIDE - 1)]
            pltpu.make_async_copy(three, three, scan_send.at[which].at[stage_index]).wait()
    for t in range(3):
        pltpu.make_async_copy(result.at[t], outs[t], final_sem.at[t]).wait()


def local(queries, key_rows, value_rows, out_grad, log_decay):
    shape = jax.ShapeDtypeStruct(queries.shape, BF16)
    anywhere = pl.BlockSpec(memory_space=pl.ANY)
    total = SLOTS * ROWS
    dma = pltpu.SemaphoreType.DMA
    return pl.pallas_call(
        kernel,
        out_shape=(shape,) * 3,
        in_specs=[anywhere] * 5,
        out_specs=(anywhere,) * 3,
        scratch_shapes=[
            pltpu.VMEM((4, ROWS, HEADS * DIM), BF16),
            pltpu.VMEM((BLOCKS, BLOCK), F32),
            pltpu.VMEM((BLOCKS, BLOCKS, BLOCK), F32),
            pltpu.VMEM((4, total, DIM), BF16),
            pltpu.VMEM((3, total, DIM), BF16),
            pltpu.VMEM((3, ROWS, HEADS * DIM), BF16),
            pltpu.VMEM((BLOCKS, BLOCK, BLOCK), F32),
            pltpu.VMEM((BLOCKS, BLOCK, DIM), F32),
            pltpu.VMEM((BLOCKS, BLOCK, DIM), F32),
            pltpu.VMEM((BLOCKS, 8, DIM), F32),
            pltpu.VMEM((BLOCKS, BLOCK, BLOCK), BF16),
            pltpu.VMEM((2, BLOCKS, DIM, DIM), F32),
            pltpu.VMEM((2, BLOCKS, STATE, DIM), F32),
            pltpu.VMEM((BLOCKS, BLOCK, DIM), F32),
            pltpu.VMEM((BLOCKS, BLOCK, DIM), F32),
            pltpu.VMEM((2, STATE, DIM), F32),
            pltpu.VMEM((2, SIDE, STATE, DIM), F32),
            pltpu.VMEM((2, STATE, DIM), F32),
            pltpu.VMEM((2, SIDE, STATE, DIM), F32),
            dma((5,)),
            dma((2,)),
            dma((4,)),
            dma((4,)),
            dma((3,)),
            dma((3,)),
            dma((2, 2)),
            dma((2, 2)),
            dma((3,)),
        ],
        compiler_params=pltpu.CompilerParams(collective_id=0, has_side_effects=True),
        name="attention_backward",
    )(queries, key_rows, value_rows, out_grad, log_decay)


def solution(mesh):
    rows = P(("seq", "head"), None)
    return jax.shard_map(
        local,
        mesh=mesh,
        in_specs=(rows, rows, rows, rows, P("head", "seq")),
        out_specs=(rows, rows, rows),
        check_vma=False,
    )
```

```python
import jax
import jax.numpy as jnp
from jax import lax
from jax.experimental import pallas as pl
from jax.experimental.pallas import tpu as pltpu
from jax.sharding import PartitionSpec as P

MESH = pl.DeviceIdType.MESH
F32 = jnp.float32
BF16 = jnp.bfloat16

DIM = 128
BLOCK = 256
ROWS = 16
LINE = 16
RING = 32
SIDE = 4
BLOCKS = 4
HEADS = 64
SLOTS = RING * 2
STATE = DIM + 8

K, V, G, Q = 0, 1, 2, 3
DQ, DK, DV = 0, 1, 2


def nt(a, b):
    return lax.dot_general(a, b, (((1,), (1,)), ((), ())), preferred_element_type=F32)


def nn(a, b):
    return lax.dot_general(a, b, (((1,), (0,)), ((), ())), preferred_element_type=F32)


def tn(a, b):
    return lax.dot_general(a, b, (((0,), (0,)), ((), ())), preferred_element_type=F32)


def kernel(
    q_in, k_in, v_in, g_in, decay_in, dq_out, dk_out, dv_out,
    stage, decay_own, decays, rows, back,
    decay_matrix, query_weight, key_weight, gates, scores,
    states, before, part_dk, part_dv,
    total_out, gather_x, row_out, gather_y,
    stage_sem, decay_sem, in_send, in_recv, out_send, out_recv, scan_send, scan_recv, left_sem, right_sem,
):
    s, z_lo = lax.axis_index("seq"), lax.axis_index("head")
    y, x, z_hi, core = s // 16, (s // 4) % 4, (s // 2) % 2, s % 2
    base = (s // 4) * 4
    z = z_hi * LINE + z_lo
    my_block = z_hi * 2 + core
    my_slot = my_block * LINE + z_lo
    my_head = z_lo * BLOCKS + my_block

    def device(zz, cc):
        return (base + (zz // LINE) * 2 + cc, zz % LINE)

    def slot_of(zz, cc):
        return ((zz // LINE) * 2 + cc) * LINE + zz % LINE

    def head_of(zz, cc):
        return (zz % LINE) * BLOCKS + (zz // LINE) * 2 + cc

    def slot_rows(slot):
        return pl.ds(pl.multiple_of(slot * ROWS, ROWS), ROWS)

    def head_cols(head):
        return pl.ds(pl.multiple_of(head * DIM, DIM), DIM)

    sources = (k_in, v_in, g_in, q_in)
    results = (dq_out, dk_out, dv_out)
    for t in range(4):
        pltpu.make_async_copy(sources[t], stage.at[t], stage_sem.at[t]).start()
    decay_load = pltpu.make_async_copy(decay_in, decay_own, stage_sem.at[4])
    decay_load.start()

    barrier = pltpu.get_barrier_semaphore()

    def greet(device_id):
        pl.semaphore_signal(barrier, inc=1, device_id=device_id, device_id_type=MESH)

    right, left = (z + 1) % RING, (z + RING - 1) % RING
    for cc in (0, 1):
        greet(device(right, cc))
        greet(device(left, cc))
    greet(device(z, 1 - core))
    for step in range(1, SIDE):
        for peer in (y * 16 + ((x + step) % SIDE) * 4, ((y + step) % SIDE) * 16 + x * 4):
            greet((peer + my_block, z_lo))
    for t in range(4):
        pltpu.make_async_copy(sources[t], stage.at[t], stage_sem.at[t]).wait()
    decay_load.wait()
    pl.semaphore_wait(barrier, 5 + 2 * (SIDE - 1))

    def exchange(send):
        def both_ways(i, carry):
            far = LINE - i
            for cc in (0, 1):
                send((z + far) % RING, cc)

            @pl.when(far < LINE)
            def _():
                for cc in (0, 1):
                    send((z + RING - far) % RING, cc)

            return carry

        lax.fori_loop(0, LINE, both_ways, 0)
        send(z, 1 - core)

    def send_input(t, zz, cc):
        pltpu.make_async_remote_copy(
            src_ref=stage.at[t].at[:, head_cols(head_of(zz, cc))],
            dst_ref=rows.at[t].at[slot_rows(my_slot)],
            send_sem=in_send.at[t],
            recv_sem=in_recv.at[t],
            device_id=device(zz, cc),
            device_id_type=MESH,
        ).start()

    def keep_input(t):
        pltpu.make_async_copy(
            stage.at[t].at[:, head_cols(my_head)], rows.at[t].at[slot_rows(my_slot)], in_recv.at[t]
        ).start()

    def farther(i, carry):
        far = i + 1

        @pl.when(far > 1)
        def _():
            pl.semaphore_wait(left_sem, 1)
            pl.semaphore_wait(right_sem, 1)

        @pl.when(far < LINE)
        def _():
            pl.semaphore_signal(left_sem, inc=1, device_id=device(right, core), device_id_type=MESH)
            pl.semaphore_signal(right_sem, inc=1, device_id=device(left, core), device_id_type=MESH)

        for t in (K, V):
            for cc in (0, 1):
                send_input(t, (z + far) % RING, cc)

            @pl.when(far < LINE)
            def _():
                for cc in (0, 1):
                    send_input(t, (z + RING - far) % RING, cc)

        return carry

    lax.fori_loop(0, LINE, farther, 0)

    def send_outputs(t):
        def send(zz, cc):
            pltpu.make_async_remote_copy(
                src_ref=back.at[t].at[slot_rows(slot_of(zz, cc))],
                dst_ref=results[t].at[:, head_cols(my_head)],
                send_sem=out_send.at[t],
                recv_sem=out_recv.at[t],
                device_id=device(zz, cc),
                device_id_type=MESH,
            ).start()

        exchange(send)
        pltpu.make_async_copy(
            back.at[t].at[slot_rows(my_slot)], results[t].at[:, head_cols(my_head)], out_recv.at[t]
        ).start()

    def arrived(t):
        pltpu.make_async_copy(rows.at[t], rows.at[t], in_recv.at[t]).wait()

    for step in range(1, BLOCKS):
        peer = (my_block + step) % BLOCKS
        pltpu.make_async_remote_copy(
            src_ref=decay_own,
            dst_ref=decays.at[my_block],
            send_sem=decay_sem.at[0],
            recv_sem=decay_sem.at[1],
            device_id=(base + peer, z_lo),
            device_id_type=MESH,
        ).start()
    pltpu.make_async_copy(decay_own, decays.at[my_block], decay_sem.at[1]).start()
    for t in (K, V):
        send_input(t, z, 1 - core)
    for t in (G, Q):
        exchange(lambda zz, cc, t=t: send_input(t, zz, cc))
    for t in range(4):
        keep_input(t)

    pltpu.make_async_copy(decays, decays, decay_sem.at[1]).wait()
    every = decays[...]
    wanted = lax.broadcasted_iota(jnp.int32, every.shape, 1) == my_block
    decay_rows = jnp.sum(jnp.where(wanted, every, 0.0), axis=1)
    upper = (
        lax.broadcasted_iota(jnp.int32, (BLOCK, BLOCK), 0)
        <= lax.broadcasted_iota(jnp.int32, (BLOCK, BLOCK), 1)
    ).astype(F32)
    padded = jnp.concatenate([decay_rows, jnp.zeros_like(decay_rows)], axis=0)
    cumulative = jnp.dot(
        padded, upper, preferred_element_type=F32, precision=lax.Precision.HIGHEST
    )
    time_at = lax.broadcasted_iota(jnp.int32, (BLOCK, DIM), 0)
    source_at = lax.broadcasted_iota(jnp.int32, (BLOCK, DIM), 1)
    for b in range(BLOCKS):
        row = cumulative[b : b + 1, :]
        column = jnp.transpose(jnp.broadcast_to(row, (DIM, BLOCK)))
        last = row[:, BLOCK - 1 : BLOCK]
        query_weight[b] = jnp.exp(column)
        key_weight[b] = jnp.exp(last - column)
        gates[b] = jnp.broadcast_to(jnp.exp(last), (8, DIM))
        for half in range(2):
            causal = time_at >= source_at + half * DIM
            spread = column - row[:, half * DIM : (half + 1) * DIM]
            decay_matrix[b, :, half * DIM : (half + 1) * DIM] = jnp.where(
                causal, jnp.exp(jnp.where(causal, spread, 0.0)), 0.0
            )

    def block(t, b):
        return rows[t, pl.ds(pl.multiple_of(b * BLOCK, BLOCK), BLOCK), :]

    def block_states(weight, left, right, which):
        def one(b, carry):
            scaled = (block(left, b).astype(F32) * weight[b]).astype(BF16)
            states[which, b] = tn(scaled, block(right, b))
            return carry

        lax.fori_loop(0, BLOCKS, one, 0)

    def scan_start(which, order):
        running = jnp.zeros((DIM, DIM), F32)
        gate = jnp.ones((8, DIM), F32)
        for b in order:
            here = gates[b]
            before[which, b, :DIM, :] = running
            before[which, b, DIM:, :] = gate
            running = here[:1] * running + states[which, b]
            gate = gate * here
        total_out[which, :DIM, :] = running
        total_out[which, DIM:, :] = gate
        gather_x[which, x, :DIM, :] = running
        gather_x[which, x, DIM:, :] = gate
        for step in range(1, SIDE):
            peer = y * 16 + ((x + step) % SIDE) * 4 + my_block
            pltpu.make_async_remote_copy(
                src_ref=total_out.at[which],
                dst_ref=gather_x.at[which].at[x],
                send_sem=scan_send.at[which].at[0],
                recv_sem=scan_recv.at[which].at[0],
                device_id=(peer, z_lo),
                device_id_type=MESH,
            ).start()

    def combined(gathered, which, place, order, backward):
        pre, pre_gate = jnp.zeros((DIM, DIM), F32), jnp.ones((8, DIM), F32)
        whole, whole_gate = pre, pre_gate
        for j in order:
            state, gate = gathered[which, j, :DIM, :], gathered[which, j, DIM:, :]
            earlier = j > place if backward else j < place
            pre = jnp.where(earlier, gate[:1] * pre + state, pre)
            pre_gate = jnp.where(earlier, gate * pre_gate, pre_gate)
            whole = gate[:1] * whole + state
            whole_gate = gate * whole_gate
        return pre, pre_gate, whole, whole_gate

    def wait_three(gathered, which, stage_index):
        three = gathered.at[which].at[pl.ds(0, SIDE - 1)]
        pltpu.make_async_copy(three, three, scan_recv.at[which].at[stage_index]).wait()

    def scan_finish(which, backward):
        order = tuple(reversed(range(SIDE))) if backward else tuple(range(SIDE))
        wait_three(gather_x, which, 0)
        pre, pre_gate, whole, whole_gate = combined(gather_x, which, x, order, backward)
        row_out[which, :DIM, :] = whole
        row_out[which, DIM:, :] = whole_gate
        gather_y[which, y, :DIM, :] = whole
        gather_y[which, y, DIM:, :] = whole_gate
        for step in range(1, SIDE):
            peer = ((y + step) % SIDE) * 16 + x * 4 + my_block
            pltpu.make_async_remote_copy(
                src_ref=row_out.at[which],
                dst_ref=gather_y.at[which].at[y],
                send_sem=scan_send.at[which].at[1],
                recv_sem=scan_recv.at[which].at[1],
                device_id=(peer, z_lo),
                device_id_type=MESH,
            ).start()
        wait_three(gather_y, which, 1)
        outer, _, _, _ = combined(gather_y, which, y, order, backward)
        return pre_gate[:1] * outer + pre

    arrived(K)
    arrived(V)
    block_states(key_weight, K, V, 0)
    scan_start(0, tuple(range(BLOCKS)))
    incoming = scan_finish(0, False)
    for b in range(BLOCKS):
        states[0, b] = before[0, b, DIM : DIM + 1, :] * incoming + before[0, b, :DIM, :]

    arrived(G)

    def query_block(b, carry):
        grad = block(G, b)
        low = (nt(grad, block(V, b)) * decay_matrix[b]).astype(BF16)
        scores[b] = low
        inner = nn(low, block(K, b))
        outer = query_weight[b] * nt(grad, states[0, b].astype(BF16))
        back[DQ, pl.ds(pl.multiple_of(b * BLOCK, BLOCK), BLOCK), :] = (inner + outer).astype(BF16)
        return carry

    lax.fori_loop(0, BLOCKS, query_block, 0)
    send_outputs(DQ)

    arrived(Q)
    block_states(query_weight, Q, G, 1)
    scan_start(1, tuple(reversed(range(BLOCKS))))

    def inner_block(b, carry):
        query, grad = block(Q, b), block(G, b)
        part_dk[b] = tn(scores[b], query)
        low = (nt(query, block(K, b)) * decay_matrix[b]).astype(BF16)
        part_dv[b] = tn(low, grad)
        return carry

    lax.fori_loop(0, BLOCKS, inner_block, 0)
    outgoing = scan_finish(1, True)
    for b in range(BLOCKS):
        states[1, b] = before[1, b, DIM : DIM + 1, :] * outgoing + before[1, b, :DIM, :]

    def key_block(b, carry):
        low = states[1, b].astype(BF16)
        grad = part_dk[b] + key_weight[b] * nt(block(V, b), low)
        back[DK, pl.ds(pl.multiple_of(b * BLOCK, BLOCK), BLOCK), :] = grad.astype(BF16)
        return carry

    lax.fori_loop(0, BLOCKS, key_block, 0)
    send_outputs(DK)

    def value_block(b, carry):
        low = states[1, b].astype(BF16)
        grad = part_dv[b] + key_weight[b] * nn(block(K, b), low)
        back[DV, pl.ds(pl.multiple_of(b * BLOCK, BLOCK), BLOCK), :] = grad.astype(BF16)
        return carry

    lax.fori_loop(0, BLOCKS, value_block, 0)
    send_outputs(DV)

    for t in range(3):
        pltpu.make_async_copy(results[t], results[t], out_recv.at[t]).wait()

    others = pl.ds(0, (SLOTS - 1) * ROWS)
    for t in range(4):
        sent = rows.at[t].at[others]
        pltpu.make_async_copy(sent, sent, in_send.at[t]).wait()
    for t in range(3):
        sent = back.at[t].at[others]
        pltpu.make_async_copy(sent, sent, out_send.at[t]).wait()
    three = decays.at[pl.ds(0, BLOCKS - 1)]
    pltpu.make_async_copy(three, three, decay_sem.at[0]).wait()
    for which in range(2):
        for stage_index, gathered in enumerate((gather_x, gather_y)):
            three = gathered.at[which].at[pl.ds(0, SIDE - 1)]
            pltpu.make_async_copy(three, three, scan_send.at[which].at[stage_index]).wait()


def place(dq_in, dk_in, dv_in, dq_out, dk_out, dv_out, sem):
    pairs = ((dq_in, dq_out), (dk_in, dk_out), (dv_in, dv_out))
    copies = [pltpu.make_async_copy(*pair, sem.at[t]) for t, pair in enumerate(pairs)]
    for copy in copies:
        copy.start()
    for copy in copies:
        copy.wait()


def local(queries, key_rows, value_rows, out_grad, log_decay):
    shape = jax.ShapeDtypeStruct(queries.shape, BF16)
    anywhere = pl.BlockSpec(memory_space=pl.ANY)
    total = SLOTS * ROWS
    dma = pltpu.SemaphoreType.DMA
    held = [
        pltpu.with_memory_space_constraint(array, pltpu.HBM)
        for array in (queries, key_rows, value_rows, out_grad, log_decay)
    ]
    grads = pl.pallas_call(
        kernel,
        out_shape=(shape,) * 3,
        in_specs=[pl.BlockSpec(memory_space=pltpu.HBM)] * 5,
        out_specs=(pl.BlockSpec(memory_space=pltpu.VMEM),) * 3,
        scratch_shapes=[
            pltpu.VMEM((4, ROWS, HEADS * DIM), BF16),
            pltpu.VMEM((BLOCKS, BLOCK), F32),
            pltpu.VMEM((BLOCKS, BLOCKS, BLOCK), F32),
            pltpu.VMEM((4, total, DIM), BF16),
            pltpu.VMEM((3, total, DIM), BF16),
            pltpu.VMEM((BLOCKS, BLOCK, BLOCK), F32),
            pltpu.VMEM((BLOCKS, BLOCK, DIM), F32),
            pltpu.VMEM((BLOCKS, BLOCK, DIM), F32),
            pltpu.VMEM((BLOCKS, 8, DIM), F32),
            pltpu.VMEM((BLOCKS, BLOCK, BLOCK), BF16),
            pltpu.VMEM((2, BLOCKS, DIM, DIM), F32),
            pltpu.VMEM((2, BLOCKS, STATE, DIM), F32),
            pltpu.VMEM((BLOCKS, BLOCK, DIM), F32),
            pltpu.VMEM((BLOCKS, BLOCK, DIM), F32),
            pltpu.VMEM((2, STATE, DIM), F32),
            pltpu.VMEM((2, SIDE, STATE, DIM), F32),
            pltpu.VMEM((2, STATE, DIM), F32),
            pltpu.VMEM((2, SIDE, STATE, DIM), F32),
            dma((5,)),
            dma((2,)),
            dma((4,)),
            dma((4,)),
            dma((3,)),
            dma((3,)),
            dma((2, 2)),
            dma((2, 2)),
            pltpu.SemaphoreType.REGULAR,
            pltpu.SemaphoreType.REGULAR,
        ],
        compiler_params=pltpu.CompilerParams(
            collective_id=0, has_side_effects=True, vmem_limit_bytes=16 * 2**20
        ),
        name="attention_backward",
    )(*held)
    return pl.pallas_call(
        place,
        out_shape=(shape,) * 3,
        in_specs=[pl.BlockSpec(memory_space=pltpu.VMEM)] * 3,
        out_specs=(anywhere,) * 3,
        scratch_shapes=[dma((3,))],
        compiler_params=pltpu.CompilerParams(vmem_limit_bytes=4 * 2**20),
        name="place",
    )(*grads)


def solution(mesh):
    rows = P(("seq", "head"), None)
    return jax.shard_map(
        local,
        mesh=mesh,
        in_specs=(rows, rows, rows, rows, P("head", "seq")),
        out_specs=(rows, rows, rows),
        check_vma=False,
    )
```

```python
import jax
import jax.numpy as jnp
from jax import lax
from jax.experimental import pallas as pl
from jax.experimental.pallas import tpu as pltpu
from jax.sharding import PartitionSpec as P

MESH = pl.DeviceIdType.MESH
F32 = jnp.float32
BF16 = jnp.bfloat16

DIM = 128
BLOCK = 256
ROWS = 16
LINE = 16
RING = 32
SIDE = 4
BLOCKS = 4
HEADS = 64
SLOTS = RING * 2
STATE = DIM + 8

K, V, G, Q = 0, 1, 2, 3
DQ, DK, DV = 0, 1, 2
EARLY = (DV,)
EDGES = (0, 1, 2, 3, 4, 6, 8, 11, 32)


def nt(a, b):
    return lax.dot_general(a, b, (((1,), (1,)), ((), ())), preferred_element_type=F32)


def nn(a, b):
    return lax.dot_general(a, b, (((1,), (0,)), ((), ())), preferred_element_type=F32)


def tn(a, b):
    return lax.dot_general(a, b, (((0,), (0,)), ((), ())), preferred_element_type=F32)


def kernel(
    q_in, k_in, v_in, g_in, decay_in, dq_out, dk_out, dv_out,
    stage, decay_own, decays, rows, back,
    decay_matrix, query_weight, key_weight, gates, scores,
    states, before, part_dk, part_dv,
    total_out, gather_x, row_out, gather_y,
    stage_sem, decay_sem, in_send, in_recv, out_send, out_recv, scan_send, scan_recv, left_sem, right_sem,
):
    s, z_lo = lax.axis_index("seq"), lax.axis_index("head")
    y, x, z_hi, core = s // 16, (s // 4) % 4, (s // 2) % 2, s % 2
    base = (s // 4) * 4
    z = z_hi * LINE + z_lo
    my_block = z_hi * 2 + core
    my_slot = my_block * LINE + z_lo
    my_head = z_lo * BLOCKS + my_block

    def device(zz, cc):
        return (base + (zz // LINE) * 2 + cc, zz % LINE)

    def slot_of(zz, cc):
        return ((zz // LINE) * 2 + cc) * LINE + zz % LINE

    def head_of(zz, cc):
        return (zz % LINE) * BLOCKS + (zz // LINE) * 2 + cc

    def slot_rows(slot):
        return pl.ds(pl.multiple_of(slot * ROWS, ROWS), ROWS)

    def head_cols(head):
        return pl.ds(pl.multiple_of(head * DIM, DIM), DIM)

    sources = (k_in, v_in, g_in, q_in)
    results = (dq_out, dk_out, dv_out)
    for t in range(4):
        pltpu.make_async_copy(sources[t], stage.at[t], stage_sem.at[t]).start()
    decay_load = pltpu.make_async_copy(decay_in, decay_own, stage_sem.at[4])
    decay_load.start()

    barrier = pltpu.get_barrier_semaphore()

    def greet(device_id):
        pl.semaphore_signal(barrier, inc=1, device_id=device_id, device_id_type=MESH)

    right, left = (z + 1) % RING, (z + RING - 1) % RING
    for cc in (0, 1):
        greet(device(right, cc))
        greet(device(left, cc))
    greet(device(z, 1 - core))
    for step in range(1, SIDE):
        for peer in (y * 16 + ((x + step) % SIDE) * 4, ((y + step) % SIDE) * 16 + x * 4):
            greet((peer + my_block, z_lo))
    for t in range(4):
        pltpu.make_async_copy(sources[t], stage.at[t], stage_sem.at[t]).wait()
    decay_load.wait()
    pl.semaphore_wait(barrier, 5 + 2 * (SIDE - 1))

    def exchange(send):
        def both_ways(i, carry):
            far = LINE - i
            for cc in (0, 1):
                send((z + far) % RING, cc)

            @pl.when(far < LINE)
            def _():
                for cc in (0, 1):
                    send((z + RING - far) % RING, cc)

            return carry

        lax.fori_loop(0, LINE, both_ways, 0)
        send(z, 1 - core)

    def early_first(send):
        for low, high in zip(EDGES[:-1], EDGES[1:]):

            def both_ways(i, carry, low=low, high=high):
                far = LINE - i
                ahead, behind = (z + far) % RING, (z + RING - far) % RING

                @pl.when((ahead >= low) & (ahead < high))
                def _():
                    for cc in (0, 1):
                        send(ahead, cc)

                @pl.when((far < LINE) & (behind >= low) & (behind < high))
                def _():
                    for cc in (0, 1):
                        send(behind, cc)

                return carry

            lax.fori_loop(0, LINE, both_ways, 0)
        send(z, 1 - core)

    def send_input(t, zz, cc):
        pltpu.make_async_remote_copy(
            src_ref=stage.at[t].at[:, head_cols(head_of(zz, cc))],
            dst_ref=rows.at[t].at[slot_rows(my_slot)],
            send_sem=in_send.at[t],
            recv_sem=in_recv.at[t],
            device_id=device(zz, cc),
            device_id_type=MESH,
        ).start()

    def keep_input(t):
        pltpu.make_async_copy(
            stage.at[t].at[:, head_cols(my_head)], rows.at[t].at[slot_rows(my_slot)], in_recv.at[t]
        ).start()

    def farther(i, carry):
        far = i + 1

        @pl.when(far > 1)
        def _():
            pl.semaphore_wait(left_sem, 1)
            pl.semaphore_wait(right_sem, 1)

        @pl.when(far < LINE)
        def _():
            pl.semaphore_signal(left_sem, inc=1, device_id=device(right, core), device_id_type=MESH)
            pl.semaphore_signal(right_sem, inc=1, device_id=device(left, core), device_id_type=MESH)

        for t in (K, V):
            for cc in (0, 1):
                send_input(t, (z + far) % RING, cc)

            @pl.when(far < LINE)
            def _():
                for cc in (0, 1):
                    send_input(t, (z + RING - far) % RING, cc)

        return carry

    lax.fori_loop(0, LINE, farther, 0)

    def send_outputs(t):
        def send(zz, cc):
            pltpu.make_async_remote_copy(
                src_ref=back.at[t].at[slot_rows(slot_of(zz, cc))],
                dst_ref=results[t].at[:, head_cols(my_head)],
                send_sem=out_send.at[t],
                recv_sem=out_recv.at[t],
                device_id=device(zz, cc),
                device_id_type=MESH,
            ).start()

        early_first(send) if t in EARLY else exchange(send)
        pltpu.make_async_copy(
            back.at[t].at[slot_rows(my_slot)], results[t].at[:, head_cols(my_head)], out_recv.at[t]
        ).start()

    def arrived(t):
        pltpu.make_async_copy(rows.at[t], rows.at[t], in_recv.at[t]).wait()

    for step in range(1, BLOCKS):
        peer = (my_block + step) % BLOCKS
        pltpu.make_async_remote_copy(
            src_ref=decay_own,
            dst_ref=decays.at[my_block],
            send_sem=decay_sem.at[0],
            recv_sem=decay_sem.at[1],
            device_id=(base + peer, z_lo),
            device_id_type=MESH,
        ).start()
    pltpu.make_async_copy(decay_own, decays.at[my_block], decay_sem.at[1]).start()
    for t in (K, V):
        send_input(t, z, 1 - core)
    for t in (G, Q):
        exchange(lambda zz, cc, t=t: send_input(t, zz, cc))
    for t in range(4):
        keep_input(t)

    pltpu.make_async_copy(decays, decays, decay_sem.at[1]).wait()
    every = decays[...]
    wanted = lax.broadcasted_iota(jnp.int32, every.shape, 1) == my_block
    decay_rows = jnp.sum(jnp.where(wanted, every, 0.0), axis=1)
    upper = (
        lax.broadcasted_iota(jnp.int32, (BLOCK, BLOCK), 0)
        <= lax.broadcasted_iota(jnp.int32, (BLOCK, BLOCK), 1)
    ).astype(F32)
    padded = jnp.concatenate([decay_rows, jnp.zeros_like(decay_rows)], axis=0)
    cumulative = jnp.dot(
        padded, upper, preferred_element_type=F32, precision=lax.Precision.HIGHEST
    )
    time_at = lax.broadcasted_iota(jnp.int32, (BLOCK, DIM), 0)
    source_at = lax.broadcasted_iota(jnp.int32, (BLOCK, DIM), 1)
    for b in range(BLOCKS):
        row = cumulative[b : b + 1, :]
        column = jnp.transpose(jnp.broadcast_to(row, (DIM, BLOCK)))
        last = row[:, BLOCK - 1 : BLOCK]
        query_weight[b] = jnp.exp(column)
        key_weight[b] = jnp.exp(last - column)
        gates[b] = jnp.broadcast_to(jnp.exp(last), (8, DIM))
        for half in range(2):
            causal = time_at >= source_at + half * DIM
            spread = column - row[:, half * DIM : (half + 1) * DIM]
            decay_matrix[b, :, half * DIM : (half + 1) * DIM] = jnp.where(
                causal, jnp.exp(jnp.where(causal, spread, 0.0)), 0.0
            )

    def block(t, b):
        return rows[t, pl.ds(pl.multiple_of(b * BLOCK, BLOCK), BLOCK), :]

    def block_states(weight, left, right, which):
        def one(b, carry):
            scaled = (block(left, b).astype(F32) * weight[b]).astype(BF16)
            states[which, b] = tn(scaled, block(right, b))
            return carry

        lax.fori_loop(0, BLOCKS, one, 0)

    def scan_start(which, order):
        running = jnp.zeros((DIM, DIM), F32)
        gate = jnp.ones((8, DIM), F32)
        for b in order:
            here = gates[b]
            before[which, b, :DIM, :] = running
            before[which, b, DIM:, :] = gate
            running = here[:1] * running + states[which, b]
            gate = gate * here
        total_out[which, :DIM, :] = running
        total_out[which, DIM:, :] = gate
        gather_x[which, x, :DIM, :] = running
        gather_x[which, x, DIM:, :] = gate
        for step in range(1, SIDE):
            peer = y * 16 + ((x + step) % SIDE) * 4 + my_block
            pltpu.make_async_remote_copy(
                src_ref=total_out.at[which],
                dst_ref=gather_x.at[which].at[x],
                send_sem=scan_send.at[which].at[0],
                recv_sem=scan_recv.at[which].at[0],
                device_id=(peer, z_lo),
                device_id_type=MESH,
            ).start()

    def combined(gathered, which, place, order, backward):
        pre, pre_gate = jnp.zeros((DIM, DIM), F32), jnp.ones((8, DIM), F32)
        whole, whole_gate = pre, pre_gate
        for j in order:
            state, gate = gathered[which, j, :DIM, :], gathered[which, j, DIM:, :]
            earlier = j > place if backward else j < place
            pre = jnp.where(earlier, gate[:1] * pre + state, pre)
            pre_gate = jnp.where(earlier, gate * pre_gate, pre_gate)
            whole = gate[:1] * whole + state
            whole_gate = gate * whole_gate
        return pre, pre_gate, whole, whole_gate

    def wait_three(gathered, which, stage_index):
        three = gathered.at[which].at[pl.ds(0, SIDE - 1)]
        pltpu.make_async_copy(three, three, scan_recv.at[which].at[stage_index]).wait()

    def scan_finish(which, backward):
        order = tuple(reversed(range(SIDE))) if backward else tuple(range(SIDE))
        wait_three(gather_x, which, 0)
        pre, pre_gate, whole, whole_gate = combined(gather_x, which, x, order, backward)
        row_out[which, :DIM, :] = whole
        row_out[which, DIM:, :] = whole_gate
        gather_y[which, y, :DIM, :] = whole
        gather_y[which, y, DIM:, :] = whole_gate
        for step in range(1, SIDE):
            peer = ((y + step) % SIDE) * 16 + x * 4 + my_block
            pltpu.make_async_remote_copy(
                src_ref=row_out.at[which],
                dst_ref=gather_y.at[which].at[y],
                send_sem=scan_send.at[which].at[1],
                recv_sem=scan_recv.at[which].at[1],
                device_id=(peer, z_lo),
                device_id_type=MESH,
            ).start()
        wait_three(gather_y, which, 1)
        outer, _, _, _ = combined(gather_y, which, y, order, backward)
        return pre_gate[:1] * outer + pre

    arrived(K)
    arrived(V)
    block_states(key_weight, K, V, 0)
    scan_start(0, tuple(range(BLOCKS)))
    incoming = scan_finish(0, False)
    for b in range(BLOCKS):
        states[0, b] = before[0, b, DIM : DIM + 1, :] * incoming + before[0, b, :DIM, :]

    arrived(G)

    def query_block(b, carry):
        grad = block(G, b)
        low = (nt(grad, block(V, b)) * decay_matrix[b]).astype(BF16)
        scores[b] = low
        inner = nn(low, block(K, b))
        outer = query_weight[b] * nt(grad, states[0, b].astype(BF16))
        back[DQ, pl.ds(pl.multiple_of(b * BLOCK, BLOCK), BLOCK), :] = (inner + outer).astype(BF16)
        return carry

    lax.fori_loop(0, BLOCKS, query_block, 0)
    send_outputs(DQ)

    arrived(Q)
    block_states(query_weight, Q, G, 1)
    scan_start(1, tuple(reversed(range(BLOCKS))))

    def inner_block(b, carry):
        query, grad = block(Q, b), block(G, b)
        part_dk[b] = tn(scores[b], query)
        low = (nt(query, block(K, b)) * decay_matrix[b]).astype(BF16)
        part_dv[b] = tn(low, grad)
        return carry

    lax.fori_loop(0, BLOCKS, inner_block, 0)
    outgoing = scan_finish(1, True)
    for b in range(BLOCKS):
        states[1, b] = before[1, b, DIM : DIM + 1, :] * outgoing + before[1, b, :DIM, :]

    def key_block(b, carry):
        low = states[1, b].astype(BF16)
        grad = part_dk[b] + key_weight[b] * nt(block(V, b), low)
        back[DK, pl.ds(pl.multiple_of(b * BLOCK, BLOCK), BLOCK), :] = grad.astype(BF16)
        return carry

    lax.fori_loop(0, BLOCKS, key_block, 0)
    send_outputs(DK)

    def value_block(b, carry):
        low = states[1, b].astype(BF16)
        grad = part_dv[b] + key_weight[b] * nn(block(K, b), low)
        back[DV, pl.ds(pl.multiple_of(b * BLOCK, BLOCK), BLOCK), :] = grad.astype(BF16)
        return carry

    lax.fori_loop(0, BLOCKS, value_block, 0)
    send_outputs(DV)

    for t in range(3):
        pltpu.make_async_copy(results[t], results[t], out_recv.at[t]).wait()

    others = pl.ds(0, (SLOTS - 1) * ROWS)
    for t in range(4):
        sent = rows.at[t].at[others]
        pltpu.make_async_copy(sent, sent, in_send.at[t]).wait()
    for t in range(3):
        sent = back.at[t].at[others]
        pltpu.make_async_copy(sent, sent, out_send.at[t]).wait()
    three = decays.at[pl.ds(0, BLOCKS - 1)]
    pltpu.make_async_copy(three, three, decay_sem.at[0]).wait()
    for which in range(2):
        for stage_index, gathered in enumerate((gather_x, gather_y)):
            three = gathered.at[which].at[pl.ds(0, SIDE - 1)]
            pltpu.make_async_copy(three, three, scan_send.at[which].at[stage_index]).wait()


def place(dq_in, dk_in, dv_in, dq_out, dk_out, dv_out, sem):
    pairs = ((dq_in, dq_out), (dk_in, dk_out), (dv_in, dv_out))
    copies = [pltpu.make_async_copy(*pair, sem.at[t]) for t, pair in enumerate(pairs)]
    for copy in copies:
        copy.start()
    for copy in copies:
        copy.wait()


def local(queries, key_rows, value_rows, out_grad, log_decay):
    shape = jax.ShapeDtypeStruct(queries.shape, BF16)
    anywhere = pl.BlockSpec(memory_space=pl.ANY)
    total = SLOTS * ROWS
    dma = pltpu.SemaphoreType.DMA
    held = [
        pltpu.with_memory_space_constraint(array, pltpu.HBM)
        for array in (queries, key_rows, value_rows, out_grad, log_decay)
    ]
    grads = pl.pallas_call(
        kernel,
        out_shape=(shape,) * 3,
        in_specs=[pl.BlockSpec(memory_space=pltpu.HBM)] * 5,
        out_specs=(pl.BlockSpec(memory_space=pltpu.VMEM),) * 3,
        scratch_shapes=[
            pltpu.VMEM((4, ROWS, HEADS * DIM), BF16),
            pltpu.VMEM((BLOCKS, BLOCK), F32),
            pltpu.VMEM((BLOCKS, BLOCKS, BLOCK), F32),
            pltpu.VMEM((4, total, DIM), BF16),
            pltpu.VMEM((3, total, DIM), BF16),
            pltpu.VMEM((BLOCKS, BLOCK, BLOCK), F32),
            pltpu.VMEM((BLOCKS, BLOCK, DIM), F32),
            pltpu.VMEM((BLOCKS, BLOCK, DIM), F32),
            pltpu.VMEM((BLOCKS, 8, DIM), F32),
            pltpu.VMEM((BLOCKS, BLOCK, BLOCK), BF16),
            pltpu.VMEM((2, BLOCKS, DIM, DIM), F32),
            pltpu.VMEM((2, BLOCKS, STATE, DIM), F32),
            pltpu.VMEM((BLOCKS, BLOCK, DIM), F32),
            pltpu.VMEM((BLOCKS, BLOCK, DIM), F32),
            pltpu.VMEM((2, STATE, DIM), F32),
            pltpu.VMEM((2, SIDE, STATE, DIM), F32),
            pltpu.VMEM((2, STATE, DIM), F32),
            pltpu.VMEM((2, SIDE, STATE, DIM), F32),
            dma((5,)),
            dma((2,)),
            dma((4,)),
            dma((4,)),
            dma((3,)),
            dma((3,)),
            dma((2, 2)),
            dma((2, 2)),
            pltpu.SemaphoreType.REGULAR,
            pltpu.SemaphoreType.REGULAR,
        ],
        compiler_params=pltpu.CompilerParams(
            collective_id=0, has_side_effects=True, vmem_limit_bytes=16 * 2**20
        ),
        name="attention_backward",
    )(*held)
    return pl.pallas_call(
        place,
        out_shape=(shape,) * 3,
        in_specs=[pl.BlockSpec(memory_space=pltpu.VMEM)] * 3,
        out_specs=(anywhere,) * 3,
        scratch_shapes=[dma((3,))],
        compiler_params=pltpu.CompilerParams(vmem_limit_bytes=4 * 2**20),
        name="place",
    )(*grads)


def solution(mesh):
    rows = P(("seq", "head"), None)
    return jax.shard_map(
        local,
        mesh=mesh,
        in_specs=(rows, rows, rows, rows, P("head", "seq")),
        out_specs=(rows, rows, rows),
        check_vma=False,
    )
```

```python
import jax
import jax.numpy as jnp
from jax import lax
from jax.experimental import pallas as pl
from jax.experimental.pallas import tpu as pltpu
from jax.sharding import PartitionSpec as P

MESH = pl.DeviceIdType.MESH
F32 = jnp.float32
BF16 = jnp.bfloat16

DIM = 128
BLOCK = 256
ROWS = 16
LINE = 16
RING = 32
SIDE = 4
BLOCKS = 4
HEADS = 64
SLOTS = RING * 2
STATE = DIM + 8

K, V, G, Q = 0, 1, 2, 3
DQ, DK, DV = 0, 1, 2
EDGES = (0, 1, 2, 3, 4, 5, 6, 8, 10)


def nt(a, b):
    return lax.dot_general(a, b, (((1,), (1,)), ((), ())), preferred_element_type=F32)


def nn(a, b):
    return lax.dot_general(a, b, (((1,), (0,)), ((), ())), preferred_element_type=F32)


def tn(a, b):
    return lax.dot_general(a, b, (((0,), (0,)), ((), ())), preferred_element_type=F32)


def kernel(
    q_in, k_in, v_in, g_in, decay_in, dq_out, dk_out, dv_out,
    stage, decay_own, decays, rows, back,
    decay_matrix, query_weight, key_weight, gates, scores,
    states, before, part_dk, part_dv,
    total_out, gather_x, row_out, gather_y,
    stage_sem, decay_sem, in_send, in_recv, out_send, out_recv, scan_send, scan_recv, left_sem, right_sem,
):
    s, z_lo = lax.axis_index("seq"), lax.axis_index("head")
    y, x, z_hi, core = s // 16, (s // 4) % 4, (s // 2) % 2, s % 2
    base = (s // 4) * 4
    z = z_hi * LINE + z_lo
    my_block = z_hi * 2 + core
    my_slot = my_block * LINE + z_lo
    my_head = z_lo * BLOCKS + my_block

    def device(zz, cc):
        return (base + (zz // LINE) * 2 + cc, zz % LINE)

    def slot_of(zz, cc):
        return ((zz // LINE) * 2 + cc) * LINE + zz % LINE

    def head_of(zz, cc):
        return (zz % LINE) * BLOCKS + (zz // LINE) * 2 + cc

    def slot_rows(slot):
        return pl.ds(pl.multiple_of(slot * ROWS, ROWS), ROWS)

    def head_cols(head):
        return pl.ds(pl.multiple_of(head * DIM, DIM), DIM)

    sources = (k_in, v_in, g_in, q_in)
    results = (dq_out, dk_out, dv_out)
    for t in range(4):
        pltpu.make_async_copy(sources[t], stage.at[t], stage_sem.at[t]).start()
    decay_load = pltpu.make_async_copy(decay_in, decay_own, stage_sem.at[4])
    decay_load.start()

    barrier = pltpu.get_barrier_semaphore()

    def greet(device_id):
        pl.semaphore_signal(barrier, inc=1, device_id=device_id, device_id_type=MESH)

    right, left = (z + 1) % RING, (z + RING - 1) % RING
    for cc in (0, 1):
        greet(device(right, cc))
        greet(device(left, cc))
    greet(device(z, 1 - core))
    for step in range(1, SIDE):
        for peer in (y * 16 + ((x + step) % SIDE) * 4, ((y + step) % SIDE) * 16 + x * 4):
            greet((peer + my_block, z_lo))
    for t in range(4):
        pltpu.make_async_copy(sources[t], stage.at[t], stage_sem.at[t]).wait()
    decay_load.wait()
    pl.semaphore_wait(barrier, 5 + 2 * (SIDE - 1))

    def exchange(send):
        def both_ways(i, carry):
            far = LINE - i
            for cc in (0, 1):
                send((z + far) % RING, cc)

            @pl.when(far < LINE)
            def _():
                for cc in (0, 1):
                    send((z + RING - far) % RING, cc)

            return carry

        lax.fori_loop(0, LINE, both_ways, 0)
        send(z, 1 - core)

    def send_input(t, zz, cc):
        pltpu.make_async_remote_copy(
            src_ref=stage.at[t].at[:, head_cols(head_of(zz, cc))],
            dst_ref=rows.at[t].at[slot_rows(my_slot)],
            send_sem=in_send.at[t],
            recv_sem=in_recv.at[t],
            device_id=device(zz, cc),
            device_id_type=MESH,
        ).start()

    def keep_input(t):
        pltpu.make_async_copy(
            stage.at[t].at[:, head_cols(my_head)], rows.at[t].at[slot_rows(my_slot)], in_recv.at[t]
        ).start()

    def farther(i, carry):
        far = i + 1

        @pl.when(far > 1)
        def _():
            pl.semaphore_wait(left_sem, 1)
            pl.semaphore_wait(right_sem, 1)

        @pl.when(far < LINE)
        def _():
            pl.semaphore_signal(left_sem, inc=1, device_id=device(right, core), device_id_type=MESH)
            pl.semaphore_signal(right_sem, inc=1, device_id=device(left, core), device_id_type=MESH)

        for t in (K, V):
            for cc in (0, 1):
                send_input(t, (z + far) % RING, cc)

            @pl.when(far < LINE)
            def _():
                for cc in (0, 1):
                    send_input(t, (z + RING - far) % RING, cc)

        return carry

    lax.fori_loop(0, LINE, farther, 0)

    def output_sender(t):
        def send(zz, cc):
            pltpu.make_async_remote_copy(
                src_ref=back.at[t].at[slot_rows(slot_of(zz, cc))],
                dst_ref=results[t].at[:, head_cols(my_head)],
                send_sem=out_send.at[t],
                recv_sem=out_recv.at[t],
                device_id=device(zz, cc),
                device_id_type=MESH,
            ).start()

        return send

    def send_range(t, low, high):
        send = output_sender(t)

        def both_ways(i, carry):
            far = LINE - i
            ahead, behind = (z + far) % RING, (z + RING - far) % RING

            @pl.when((ahead >= low) & (ahead < high))
            def _():
                for cc in (0, 1):
                    send(ahead, cc)

            @pl.when((far < LINE) & (behind >= low) & (behind < high))
            def _():
                for cc in (0, 1):
                    send(behind, cc)

            return carry

        lax.fori_loop(0, LINE, both_ways, 0)

    def keep_output(t):
        output_sender(t)(z, 1 - core)
        pltpu.make_async_copy(
            back.at[t].at[slot_rows(my_slot)], results[t].at[:, head_cols(my_head)], out_recv.at[t]
        ).start()

    def arrived(t):
        pltpu.make_async_copy(rows.at[t], rows.at[t], in_recv.at[t]).wait()

    for step in range(1, BLOCKS):
        peer = (my_block + step) % BLOCKS
        pltpu.make_async_remote_copy(
            src_ref=decay_own,
            dst_ref=decays.at[my_block],
            send_sem=decay_sem.at[0],
            recv_sem=decay_sem.at[1],
            device_id=(base + peer, z_lo),
            device_id_type=MESH,
        ).start()
    pltpu.make_async_copy(decay_own, decays.at[my_block], decay_sem.at[1]).start()
    for t in (K, V):
        send_input(t, z, 1 - core)
    for t in (G, Q):
        exchange(lambda zz, cc, t=t: send_input(t, zz, cc))
    for t in range(4):
        keep_input(t)

    pltpu.make_async_copy(decays, decays, decay_sem.at[1]).wait()
    every = decays[...]
    wanted = lax.broadcasted_iota(jnp.int32, every.shape, 1) == my_block
    decay_rows = jnp.sum(jnp.where(wanted, every, 0.0), axis=1)
    upper = (
        lax.broadcasted_iota(jnp.int32, (BLOCK, BLOCK), 0)
        <= lax.broadcasted_iota(jnp.int32, (BLOCK, BLOCK), 1)
    ).astype(F32)
    padded = jnp.concatenate([decay_rows, jnp.zeros_like(decay_rows)], axis=0)
    cumulative = jnp.dot(
        padded, upper, preferred_element_type=F32, precision=lax.Precision.HIGHEST
    )
    time_at = lax.broadcasted_iota(jnp.int32, (BLOCK, DIM), 0)
    source_at = lax.broadcasted_iota(jnp.int32, (BLOCK, DIM), 1)
    for b in range(BLOCKS):
        row = cumulative[b : b + 1, :]
        column = jnp.transpose(jnp.broadcast_to(row, (DIM, BLOCK)))
        last = row[:, BLOCK - 1 : BLOCK]
        query_weight[b] = jnp.exp(column)
        key_weight[b] = jnp.exp(last - column)
        gates[b] = jnp.broadcast_to(jnp.exp(last), (8, DIM))
        for half in range(2):
            causal = time_at >= source_at + half * DIM
            spread = column - row[:, half * DIM : (half + 1) * DIM]
            decay_matrix[b, :, half * DIM : (half + 1) * DIM] = jnp.where(
                causal, jnp.exp(jnp.where(causal, spread, 0.0)), 0.0
            )

    def block(t, b):
        return rows[t, pl.ds(pl.multiple_of(b * BLOCK, BLOCK), BLOCK), :]

    def block_states(weight, left, right, which):
        def one(b, carry):
            scaled = (block(left, b).astype(F32) * weight[b]).astype(BF16)
            states[which, b] = tn(scaled, block(right, b))
            return carry

        lax.fori_loop(0, BLOCKS, one, 0)

    def scan_start(which, order):
        running = jnp.zeros((DIM, DIM), F32)
        gate = jnp.ones((8, DIM), F32)
        for b in order:
            here = gates[b]
            before[which, b, :DIM, :] = running
            before[which, b, DIM:, :] = gate
            running = here[:1] * running + states[which, b]
            gate = gate * here
        total_out[which, :DIM, :] = running
        total_out[which, DIM:, :] = gate
        gather_x[which, x, :DIM, :] = running
        gather_x[which, x, DIM:, :] = gate
        for step in range(1, SIDE):
            peer = y * 16 + ((x + step) % SIDE) * 4 + my_block
            pltpu.make_async_remote_copy(
                src_ref=total_out.at[which],
                dst_ref=gather_x.at[which].at[x],
                send_sem=scan_send.at[which].at[0],
                recv_sem=scan_recv.at[which].at[0],
                device_id=(peer, z_lo),
                device_id_type=MESH,
            ).start()

    def combined(gathered, which, place, order, backward):
        pre, pre_gate = jnp.zeros((DIM, DIM), F32), jnp.ones((8, DIM), F32)
        whole, whole_gate = pre, pre_gate
        for j in order:
            state, gate = gathered[which, j, :DIM, :], gathered[which, j, DIM:, :]
            earlier = j > place if backward else j < place
            pre = jnp.where(earlier, gate[:1] * pre + state, pre)
            pre_gate = jnp.where(earlier, gate * pre_gate, pre_gate)
            whole = gate[:1] * whole + state
            whole_gate = gate * whole_gate
        return pre, pre_gate, whole, whole_gate

    def wait_three(gathered, which, stage_index):
        three = gathered.at[which].at[pl.ds(0, SIDE - 1)]
        pltpu.make_async_copy(three, three, scan_recv.at[which].at[stage_index]).wait()

    def scan_finish(which, backward):
        order = tuple(reversed(range(SIDE))) if backward else tuple(range(SIDE))
        wait_three(gather_x, which, 0)
        pre, pre_gate, whole, whole_gate = combined(gather_x, which, x, order, backward)
        row_out[which, :DIM, :] = whole
        row_out[which, DIM:, :] = whole_gate
        gather_y[which, y, :DIM, :] = whole
        gather_y[which, y, DIM:, :] = whole_gate
        for step in range(1, SIDE):
            peer = ((y + step) % SIDE) * 16 + x * 4 + my_block
            pltpu.make_async_remote_copy(
                src_ref=row_out.at[which],
                dst_ref=gather_y.at[which].at[y],
                send_sem=scan_send.at[which].at[1],
                recv_sem=scan_recv.at[which].at[1],
                device_id=(peer, z_lo),
                device_id_type=MESH,
            ).start()
        wait_three(gather_y, which, 1)
        outer, _, _, _ = combined(gather_y, which, y, order, backward)
        return pre_gate[:1] * outer + pre

    arrived(K)
    arrived(V)
    block_states(key_weight, K, V, 0)
    scan_start(0, tuple(range(BLOCKS)))
    incoming = scan_finish(0, False)
    for b in range(BLOCKS):
        states[0, b] = before[0, b, DIM : DIM + 1, :] * incoming + before[0, b, :DIM, :]

    arrived(G)

    def query_block(b, carry):
        grad = block(G, b)
        low = (nt(grad, block(V, b)) * decay_matrix[b]).astype(BF16)
        scores[b] = low
        inner = nn(low, block(K, b))
        outer = query_weight[b] * nt(grad, states[0, b].astype(BF16))
        back[DQ, pl.ds(pl.multiple_of(b * BLOCK, BLOCK), BLOCK), :] = (inner + outer).astype(BF16)
        return carry

    lax.fori_loop(0, BLOCKS, query_block, 0)
    send_range(DQ, 0, RING)
    keep_output(DQ)

    arrived(Q)
    block_states(query_weight, Q, G, 1)
    scan_start(1, tuple(reversed(range(BLOCKS))))

    def inner_block(b, carry):
        query, grad = block(Q, b), block(G, b)
        part_dk[b] = tn(scores[b], query)
        low = (nt(query, block(K, b)) * decay_matrix[b]).astype(BF16)
        part_dv[b] = tn(low, grad)
        return carry

    lax.fori_loop(0, BLOCKS, inner_block, 0)
    outgoing = scan_finish(1, True)
    for b in range(BLOCKS):
        states[1, b] = before[1, b, DIM : DIM + 1, :] * outgoing + before[1, b, :DIM, :]

    def key_block(b, carry):
        low = states[1, b].astype(BF16)
        grad = part_dk[b] + key_weight[b] * nt(block(V, b), low)
        back[DK, pl.ds(pl.multiple_of(b * BLOCK, BLOCK), BLOCK), :] = grad.astype(BF16)
        return carry

    lax.fori_loop(0, BLOCKS, key_block, 0)
    @pl.when(z_hi == 0)
    def _():
        send_range(DK, 0, RING)

    @pl.when(z_hi == 1)
    def _():
        send_range(DK, 0, LINE)

    keep_output(DK)

    def value_block(b, carry):
        low = states[1, b].astype(BF16)
        grad = part_dv[b] + key_weight[b] * nn(block(K, b), low)
        back[DV, pl.ds(pl.multiple_of(b * BLOCK, BLOCK), BLOCK), :] = grad.astype(BF16)
        return carry

    lax.fori_loop(0, BLOCKS, value_block, 0)
    for low, high in zip(EDGES[:-1], EDGES[1:]):
        send_range(DV, low, high)

    @pl.when(z_hi == 0)
    def _():
        send_range(DV, EDGES[-1], RING)

    @pl.when(z_hi == 1)
    def _():
        send_range(DK, LINE, RING)
        send_range(DV, EDGES[-1], RING)

    keep_output(DV)

    for t in range(3):
        pltpu.make_async_copy(results[t], results[t], out_recv.at[t]).wait()

    others = pl.ds(0, (SLOTS - 1) * ROWS)
    for t in range(4):
        sent = rows.at[t].at[others]
        pltpu.make_async_copy(sent, sent, in_send.at[t]).wait()
    for t in range(3):
        sent = back.at[t].at[others]
        pltpu.make_async_copy(sent, sent, out_send.at[t]).wait()
    three = decays.at[pl.ds(0, BLOCKS - 1)]
    pltpu.make_async_copy(three, three, decay_sem.at[0]).wait()
    for which in range(2):
        for stage_index, gathered in enumerate((gather_x, gather_y)):
            three = gathered.at[which].at[pl.ds(0, SIDE - 1)]
            pltpu.make_async_copy(three, three, scan_send.at[which].at[stage_index]).wait()


def place(dq_in, dk_in, dv_in, dq_out, dk_out, dv_out, sem):
    pairs = ((dq_in, dq_out), (dk_in, dk_out), (dv_in, dv_out))
    copies = [pltpu.make_async_copy(*pair, sem.at[t]) for t, pair in enumerate(pairs)]
    for copy in copies:
        copy.start()
    for copy in copies:
        copy.wait()


def local(queries, key_rows, value_rows, out_grad, log_decay):
    shape = jax.ShapeDtypeStruct(queries.shape, BF16)
    anywhere = pl.BlockSpec(memory_space=pl.ANY)
    total = SLOTS * ROWS
    dma = pltpu.SemaphoreType.DMA
    held = [
        pltpu.with_memory_space_constraint(array, pltpu.HBM)
        for array in (queries, key_rows, value_rows, out_grad, log_decay)
    ]
    grads = pl.pallas_call(
        kernel,
        out_shape=(shape,) * 3,
        in_specs=[pl.BlockSpec(memory_space=pltpu.HBM)] * 5,
        out_specs=(pl.BlockSpec(memory_space=pltpu.VMEM),) * 3,
        scratch_shapes=[
            pltpu.VMEM((4, ROWS, HEADS * DIM), BF16),
            pltpu.VMEM((BLOCKS, BLOCK), F32),
            pltpu.VMEM((BLOCKS, BLOCKS, BLOCK), F32),
            pltpu.VMEM((4, total, DIM), BF16),
            pltpu.VMEM((3, total, DIM), BF16),
            pltpu.VMEM((BLOCKS, BLOCK, BLOCK), F32),
            pltpu.VMEM((BLOCKS, BLOCK, DIM), F32),
            pltpu.VMEM((BLOCKS, BLOCK, DIM), F32),
            pltpu.VMEM((BLOCKS, 8, DIM), F32),
            pltpu.VMEM((BLOCKS, BLOCK, BLOCK), BF16),
            pltpu.VMEM((2, BLOCKS, DIM, DIM), F32),
            pltpu.VMEM((2, BLOCKS, STATE, DIM), F32),
            pltpu.VMEM((BLOCKS, BLOCK, DIM), F32),
            pltpu.VMEM((BLOCKS, BLOCK, DIM), F32),
            pltpu.VMEM((2, STATE, DIM), F32),
            pltpu.VMEM((2, SIDE, STATE, DIM), F32),
            pltpu.VMEM((2, STATE, DIM), F32),
            pltpu.VMEM((2, SIDE, STATE, DIM), F32),
            dma((5,)),
            dma((2,)),
            dma((4,)),
            dma((4,)),
            dma((3,)),
            dma((3,)),
            dma((2, 2)),
            dma((2, 2)),
            pltpu.SemaphoreType.REGULAR,
            pltpu.SemaphoreType.REGULAR,
        ],
        compiler_params=pltpu.CompilerParams(
            collective_id=0, has_side_effects=True, vmem_limit_bytes=16 * 2**20
        ),
        name="attention_backward",
    )(*held)
    return pl.pallas_call(
        place,
        out_shape=(shape,) * 3,
        in_specs=[pl.BlockSpec(memory_space=pltpu.VMEM)] * 3,
        out_specs=(anywhere,) * 3,
        scratch_shapes=[dma((3,))],
        compiler_params=pltpu.CompilerParams(vmem_limit_bytes=4 * 2**20),
        name="place",
    )(*grads)


def solution(mesh):
    rows = P(("seq", "head"), None)
    return jax.shard_map(
        local,
        mesh=mesh,
        in_specs=(rows, rows, rows, rows, P("head", "seq")),
        out_specs=(rows, rows, rows),
        check_vma=False,
    )
```
